32 devices in a mesh: grp: 2 (over x), tok: 8 (over z, y), lay: 2 (over core).
Axes of the slice: x: 2, y: 2, z: 4, core: 2. Of those that a mesh axis runs over, the one named last changes fastest.
Arguments:
- acts: bfloat16 [3072, 16, 128], P(('grp', 'tok'), 'lay'), parts along dimension 0, may hold values from -0.5 to 0.5
- grads: bfloat16 [3072, 16, 128], P(('grp', 'tok'), 'lay'), parts along dimension 0, may hold values from -0.5 to 0.5
- losses: bfloat16 [3072, 128], P(('grp', 'tok')), parts along dimension 0, may hold values from -6 to 6
- sources: int32 [3072], P(('grp', 'tok')), parts along dimension 0, may hold values from 0 to 7
Outputs:
- scores: float32 [3072, 128], P(('grp', 'tok', 'lay')), parts along dimension 0
The draws below stay inside these ranges and needn't reach their ends.
There are 2 independent parts, one for each index of `grp`. The reference program is written for one: setup_inputs(seed, part) draws one part's arguments, and reference() takes and returns one part's arrays. A program takes and returns all parts, laid end to end along the dimension named above; each array names one. Nothing has to cross between parts.
All inputs are finite; a program needn't handle non-finite values.
Results may differ from the reference program's by a relative error of at most 0.011.
Values may be sent and summed in bfloat16 or wider, within the bound.
A program may use at most 128 MiB of HBM per device.

```python
import jax
import jax.numpy as jnp
from jax import lax

K = 128
DOM = 128
LAYERS = 16
SOURCES = 8
TOKENS = 1536


def plant(drawn, rng, least, high):
    spot = [jax.random.randint(jax.random.fold_in(rng, axis), (), 0, length) for axis, length in enumerate(drawn.shape)]
    longest = drawn.shape.index(max(drawn.shape))
    beside = spot[:longest] + [(spot[longest] + 1) % drawn.shape[longest]] + spot[longest + 1:]
    return drawn.at[tuple(spot)].set(least).at[tuple(beside)].set(high)


def levels(rng, extent, pieces, smallest, high):
    def one(position, parts):
        heights = jax.random.uniform(jax.random.fold_in(jax.random.fold_in(rng, 6), position), (parts,), jnp.float32, smallest / len(pieces), high / len(pieces))
        return jnp.repeat(jnp.exp(heights), extent[position] // parts).reshape((-1,) + (1,) * (len(extent) - position - 1))

    level = one(*pieces[0])
    for cut in pieces[1:]:
        level = level * one(*cut)
    return level


def scatter_about(own_key, dims, scale, limit, shards=(), dtype=jnp.bfloat16):
    values = scale * jax.random.normal(own_key, dims, jnp.float32)
    if shards:
        values = values * levels(own_key, dims, shards, -0.22, 0.18)
    return jnp.clip(values, -limit, limit).astype(dtype)


def setup_inputs(seed: int = 0, part: int = 0) -> dict:
    arg_keys = jax.random.split(jax.random.key(seed), 5)
    own_keys = jax.random.split(jax.random.fold_in(arg_keys[4], part), 5)
    return {
        "acts": scatter_about(own_keys[0], (TOKENS, LAYERS, K), (K ** -0.5), 0.5, ((0, 8), (1, 2))),
        "grads": scatter_about(own_keys[1], (TOKENS, LAYERS, K), (K ** -0.5), 0.5, ((0, 8), (1, 2))),
        "losses": scatter_about(own_keys[2], (TOKENS, DOM), 1.0, 6.0, ((0, 8),)),
        "sources": plant(jax.random.randint(own_keys[3], (TOKENS,), 0, SOURCES), jax.random.fold_in(own_keys[3], 1), 0, SOURCES - 1).astype(jnp.int32),
    }


def reference(acts, grads, losses, sources):
    influence = jnp.zeros((TOKENS, TOKENS), jnp.float32)
    for layer in range(LAYERS):
        act_layer = acts[:, layer, :].astype(jnp.float32)
        grad_layer = grads[:, layer, :].astype(jnp.float32)
        gram_act = jnp.dot(act_layer, act_layer.T, precision=lax.Precision.HIGHEST)
        gram_grad = jnp.dot(grad_layer, grad_layer.T, precision=lax.Precision.HIGHEST)
        influence = influence + gram_act * gram_grad
    keep = sources[:, None] != sources[None, :]
    masked = jnp.where(keep, influence, jnp.zeros_like(influence)).astype(jnp.bfloat16)
    scale = 1.0 / jnp.sqrt(jnp.float32(TOKENS * LAYERS))
    return jnp.dot(masked, losses, preferred_element_type=jnp.float32) * scale
```

```python
import functools
import math

import jax
import jax.numpy as jnp
from jax import lax
from jax.experimental import pallas as pl
from jax.experimental.pallas import tpu as pltpu
from jax.sharding import PartitionSpec as P

MESH = pl.DeviceIdType.MESH
F32 = jnp.float32
BF16 = jnp.bfloat16
GROUP = 2


def nt(a, b):
    return lax.dot_general(a, b, (((1,), (1,)), ((), ())), preferred_element_type=F32)


def kernel(
    n, lh, scale,
    acts, grads, losses, sources, out,
    stage, send, recv, lall, srcs, total, xsend, xrecv, rsend, rrecv,
    send_sem, recv_sem, ls_sem, lr_sem, lf_sem, lx_sem, ly_sem, ss_sem, sr_sem,
    xs_sem, xr_sem, rs_sem, rr_sem,
):
    block = acts.shape[0]
    half = block // 2
    sets = n // lh
    me = lax.axis_index("tok")
    h = lax.axis_index("lay")
    q, j = me // lh, lax.rem(me, lh)

    def dest(k):
        return lax.rem(q + sets - k // lh, sets) * lh + jnp.bitwise_xor(j, k % lh)

    mine = pl.ds(pl.multiple_of(h * half, half), half)
    theirs = pl.ds(pl.multiple_of((1 - h) * half, half), half)
    peers = list(range(1, n))
    order = sorted(range(1, lh), key=lambda k: (-(k.bit_length()), k))
    send_order = [kq * lh + kj for kj in order for kq in range(sets)] + [kq * lh for kq in range(1, sets)]

    barrier = pltpu.get_barrier_semaphore()
    for k in peers:
        pl.semaphore_signal(barrier, inc=1, device_id={"tok": dest(k)}, device_id_type=MESH)
    pl.semaphore_signal(barrier, inc=1, device_id={"lay": 1 - h}, device_id_type=MESH)

    for w, ref in enumerate((acts, grads)):
        stage[w] = ref[...].astype(F32).reshape(block * lh, ref.shape[2])
    lall[0] = losses[...]
    srcs[0] = sources[...]
    pl.semaphore_wait(barrier, n)

    def remote(src, dst, s, r, **where):
        return pltpu.make_async_remote_copy(
            src_ref=src, dst_ref=dst, send_sem=s, recv_sem=r, device_id=where, device_id_type=MESH
        )

    copies = []

    def go(copy):
        copy.start()
        copies.append(copy)
        return copy

    first = {}
    for k in send_order:
        if k % 2 == 0:
            first[k] = go(remote(losses.at[mine], lall.at[k, mine], ls_sem.at[k], lr_sem.at[k], tok=dest(k)))
    first[1] = go(remote(losses.at[mine], lall.at[1, mine], ls_sem.at[1], lr_sem.at[1], tok=dest(1)))
    ids = {}
    for k in send_order:
        ids[k] = go(remote(sources, srcs.at[k], ss_sem.at[k], sr_sem.at[k], tok=dest(k)))
    main = {}
    for kj in order + [0]:
        layer = jnp.bitwise_xor(j, kj)
        for w in range(2):
            piece = stage[w, pl.ds(layer, block, stride=lh), :].astype(BF16)
            send[kj, w] = piece
            if kj == 0:
                recv[0, w] = piece
        for kq in range(sets):
            k = kq * lh + kj
            if k:
                main[k] = go(remote(send.at[kj], recv.at[k], send_sem.at[k], recv_sem.at[k], tok=dest(k)))

    cross = {}
    for k in range(1, n):
        if k % 2 == 0:
            first[k].wait_recv()
            first[k + 1] = go(
                remote(lall.at[k, mine], lall.at[k + 1, mine], lf_sem.at[k + 1], lr_sem.at[k + 1], tok=dest(1))
            )
            cross[k] = go(remote(lall.at[k, mine], lall.at[k, mine], lx_sem.at[k], ly_sem.at[k], lay=1 - h))
    for k in range(1, n):
        if k % 2 == 1:
            first[k].wait_recv()
            cross[k] = go(remote(lall.at[k, mine], lall.at[k, mine], lx_sem.at[k], ly_sem.at[k], lay=1 - h))

    size = GROUP * block
    flat = (size, acts.shape[2])

    def part(ref_slice):
        return ref_slice.reshape(flat)

    def arrive(g):
        for k in range(g * GROUP, (g + 1) * GROUP):
            if k:
                main[k].wait_recv()
                ids[k].wait_recv()
                cross[k].wait_recv()

    def row_ids(g):
        return jnp.concatenate([srcs[g * GROUP + i] for i in range(GROUP)], axis=1)

    rows = {}
    cols = {}

    def one(a, b):
        sa, sb = pl.ds(a * GROUP, GROUP), pl.ds(b * GROUP, GROUP)
        x = nt(part(recv[sa, 0]), part(recv[sb, 0])) * nt(part(recv[sa, 1]), part(recv[sb, 1]))
        col = cols[a]
        reps = size // col.shape[1]
        keep = jnp.concatenate([col] * reps, axis=1) != rows[b]
        x = jnp.where(keep, x, 0.0).astype(BF16)
        return jnp.dot(x, lall[sb].reshape(size, losses.shape[1]), preferred_element_type=F32)

    groups = lh // GROUP
    for g in range(groups):
        arrive(g)
        rows[g] = row_ids(g)
        cols[g] = jnp.broadcast_to(rows[g], (128, size)).T
        acc = one(g, 0)
        for b in range(1, g + 1):
            acc = acc + one(g, b)
        total[pl.ds(g * GROUP, GROUP)] = acc.reshape(GROUP, block, losses.shape[1])
        for a in range(g):
            total[pl.ds(a * GROUP, GROUP)] += one(a, g).reshape(GROUP, block, losses.shape[1])
    for g in range(groups, n // GROUP):
        arrive(g)
    if sets > 1:
        for a in range(groups):
            cols[a] = cols[a]

        @pl.loop(groups, n // GROUP)
        def _(g):
            rows[-1] = jnp.concatenate([srcs[g * GROUP + i] for i in range(GROUP)], axis=1)
            sb = pl.ds(g * GROUP, GROUP)
            for a in range(groups):
                sa = pl.ds(a * GROUP, GROUP)
                x = nt(part(recv[sa, 0]), part(recv[sb, 0])) * nt(part(recv[sa, 1]), part(recv[sb, 1]))
                col = jnp.broadcast_to(row_ids(a), (128, size)).T
                keep = jnp.concatenate([col] * (size // 128), axis=1) != rows[-1]
                x = jnp.where(keep, x, 0.0).astype(BF16)
                y = jnp.dot(x, lall[sb].reshape(size, losses.shape[1]), preferred_element_type=F32)
                total[sa] += y.reshape(GROUP, block, losses.shape[1])

    xsend[...] = total[:, theirs].astype(BF16)
    swap = go(remote(xsend, xrecv, xs_sem, xr_sem, lay=1 - h))
    swap.wait_recv()
    back = []
    for kj in order:
        rsend[kj] = (total[kj, mine] + xrecv[kj].astype(F32)).astype(BF16)
        back.append(
            go(remote(rsend.at[kj], rrecv.at[kj], rs_sem.at[kj], rr_sem.at[kj], tok=dest(kj)))
        )
    acc = total[0, mine] + xrecv[0].astype(F32)
    for kj, copy in zip(order, back):
        copy.wait_recv()
        acc = acc + rrecv[kj].astype(F32)
    out[...] = acc * scale
    for copy in copies:
        copy.wait_send()


def on_device(acts, grads, losses, sources):
    block, lh, width = acts.shape
    dom = losses.shape[1]
    n = lax.axis_size("tok")
    layers = lh * lax.axis_size("lay")
    scale = 1.0 / math.sqrt(n * block * layers)
    half = block // 2
    dma = pltpu.SemaphoreType.DMA
    vmem = pl.BlockSpec(memory_space=pltpu.VMEM)
    pairs = n * block * block * lh
    return pl.pallas_call(
        functools.partial(kernel, n, lh, scale),
        out_shape=jax.ShapeDtypeStruct((half, dom), F32),
        in_specs=[vmem] * 4,
        out_specs=vmem,
        scratch_shapes=[
            pltpu.VMEM((2, block * lh, width), F32),
            pltpu.VMEM((lh, 2, block, width), BF16),
            pltpu.VMEM((n, 2, block, width), BF16),
            pltpu.VMEM((n, block, dom), BF16),
            pltpu.VMEM((n, 1, block), jnp.int32),
            pltpu.VMEM((lh, block, dom), F32),
            pltpu.VMEM((lh, half, dom), BF16),
            pltpu.VMEM((lh, half, dom), BF16),
            pltpu.VMEM((lh, half, dom), BF16),
            pltpu.VMEM((lh, half, dom), BF16),
            dma((n,)), dma((n,)), dma((n,)), dma((n,)), dma((n,)), dma((n,)), dma((n,)), dma((n,)), dma((n,)),
            dma, dma, dma((lh,)), dma((lh,)),
        ],
        compiler_params=pltpu.CompilerParams(
            collective_id=0, has_side_effects=True, vmem_limit_bytes=56 * 1024 * 1024
        ),
        cost_estimate=pl.CostEstimate(
            flops=2 * pairs * (2 * width + dom), bytes_accessed=4 * block * lh * width, transcendentals=0
        ),
    )(acts, grads, losses, sources.reshape(1, block))


def solution(mesh):
    placed = (
        P(("grp", "tok"), "lay", None),
        P(("grp", "tok"), "lay", None),
        P(("grp", "tok"), None),
        P(("grp", "tok")),
    )
    return jax.shard_map(
        on_device,
        mesh=mesh,
        in_specs=placed,
        out_specs=P(("grp", "tok", "lay"), None),
        check_vma=False,
    )
```

```python
import functools
import math

import jax
import jax.numpy as jnp
from jax import lax
from jax.experimental import pallas as pl
from jax.experimental.pallas import tpu as pltpu
from jax.sharding import PartitionSpec as P

MESH = pl.DeviceIdType.MESH
F32 = jnp.float32
BF16 = jnp.bfloat16
GROUP = 2


def nt(a, b):
    return lax.dot_general(a, b, (((1,), (1,)), ((), ())), preferred_element_type=F32)


def kernel(
    n, lh, scale,
    acts, grads, losses, sources, out,
    fetched, stage, send, recv, lall, srcs, total, xsend, xrecv, rsend, rrecv,
    send_sem, recv_sem, ls_sem, lr_sem, lf_sem, lx_sem, ly_sem, ss_sem, sr_sem,
    xs_sem, xr_sem, rs_sem, rr_sem, in_sem,
):
    block = acts.shape[0]
    half = block // 2
    sets = n // lh
    me = lax.axis_index("tok")
    h = lax.axis_index("lay")
    q, j = me // lh, lax.rem(me, lh)

    def dest(k):
        return lax.rem(q + sets - k // lh, sets) * lh + jnp.bitwise_xor(j, k % lh)

    mine = pl.ds(pl.multiple_of(h * half, half), half)
    theirs = pl.ds(pl.multiple_of((1 - h) * half, half), half)
    peers = list(range(1, n))
    order = sorted(range(1, lh), key=lambda k: (-(k.bit_length()), k))
    send_order = [kq * lh + kj for kj in order for kq in range(sets)] + [kq * lh for kq in range(1, sets)]

    barrier = pltpu.get_barrier_semaphore()
    for k in peers:
        pl.semaphore_signal(barrier, inc=1, device_id={"tok": dest(k)}, device_id_type=MESH)
    pl.semaphore_signal(barrier, inc=1, device_id={"lay": 1 - h}, device_id_type=MESH)

    local = [
        pltpu.make_async_copy(src, dst, in_sem.at[i])
        for i, (src, dst) in enumerate(
            ((acts, fetched.at[0]), (grads, fetched.at[1]), (losses, lall.at[0]), (sources, srcs.at[0]))
        )
    ]
    for copy in local:
        copy.start()

    def cut(kj):
        layer = jnp.bitwise_xor(j, kj)
        for w in range(2):
            piece = stage[w, pl.ds(layer, block, stride=lh), :].astype(BF16)
            if kj == 0:
                recv[0, w] = piece
            if kj or sets > 1:
                send[kj, w] = piece

    ready = order[: lh // 2]
    for w in range(2):
        local[w].wait()
        stage[w] = fetched[w].astype(F32).reshape(block * lh, acts.shape[2])
    for kj in ready:
        cut(kj)
    for copy in local[2:]:
        copy.wait()
    pl.semaphore_wait(barrier, n)

    def remote(src, dst, s, r, **where):
        return pltpu.make_async_remote_copy(
            src_ref=src, dst_ref=dst, send_sem=s, recv_sem=r, device_id=where, device_id_type=MESH
        )

    copies = []

    def go(copy):
        copy.start()
        copies.append(copy)
        return copy

    first = {}
    for k in send_order:
        if k % 2 == 0:
            first[k] = go(remote(lall.at[0, mine], lall.at[k, mine], ls_sem.at[k], lr_sem.at[k], tok=dest(k)))
    first[1] = go(remote(lall.at[0, mine], lall.at[1, mine], ls_sem.at[1], lr_sem.at[1], tok=dest(1)))
    ids = {}
    for k in send_order:
        ids[k] = go(remote(srcs.at[0], srcs.at[k], ss_sem.at[k], sr_sem.at[k], tok=dest(k)))
    main = {}
    for kj in order + [0]:
        if kj not in ready:
            cut(kj)
        for kq in range(sets):
            k = kq * lh + kj
            if k:
                main[k] = go(remote(send.at[kj], recv.at[k], send_sem.at[k], recv_sem.at[k], tok=dest(k)))

    cross = {}
    for k in range(1, n):
        if k % 2 == 0:
            first[k].wait_recv()
            first[k + 1] = go(
                remote(lall.at[k, mine], lall.at[k + 1, mine], lf_sem.at[k + 1], lr_sem.at[k + 1], tok=dest(1))
            )
            cross[k] = go(remote(lall.at[k, mine], lall.at[k, mine], lx_sem.at[k], ly_sem.at[k], lay=1 - h))
    for k in range(1, n):
        if k % 2 == 1:
            first[k].wait_recv()
            cross[k] = go(remote(lall.at[k, mine], lall.at[k, mine], lx_sem.at[k], ly_sem.at[k], lay=1 - h))

    size = GROUP * block
    flat = (size, acts.shape[2])

    def part(ref_slice):
        return ref_slice.reshape(flat)

    def arrive(g):
        for k in range(g * GROUP, (g + 1) * GROUP):
            if k:
                main[k].wait_recv()
                ids[k].wait_recv()
                cross[k].wait_recv()

    def row_ids(g):
        return jnp.concatenate([srcs[g * GROUP + i] for i in range(GROUP)], axis=1)

    rows = {}
    cols = {}

    def one(a, b):
        sa, sb = pl.ds(a * GROUP, GROUP), pl.ds(b * GROUP, GROUP)
        x = nt(part(recv[sa, 0]), part(recv[sb, 0])) * nt(part(recv[sa, 1]), part(recv[sb, 1]))
        col = cols[a]
        reps = size // col.shape[1]
        keep = jnp.concatenate([col] * reps, axis=1) != rows[b]
        x = jnp.where(keep, x, 0.0).astype(BF16)
        return jnp.dot(x, lall[sb].reshape(size, losses.shape[1]), preferred_element_type=F32)

    dom = losses.shape[1]

    def add(a, b):
        total[pl.ds(a * GROUP, GROUP)] += one(a, b).reshape(GROUP, block, dom)

    swaps = {}
    back = {}

    def swap(a):
        at = pl.ds(a * GROUP, GROUP)
        xsend[at] = total[at, theirs].astype(BF16)
        swaps[a] = go(remote(xsend.at[at], xrecv.at[at], xs_sem.at[a], xr_sem.at[a], lay=1 - h))

    def owners(a):
        swaps[a].wait_recv()
        for k in range(a * GROUP, (a + 1) * GROUP):
            if k:
                rsend[k] = (total[k, mine] + xrecv[k].astype(F32)).astype(BF16)
                back[k] = go(remote(rsend.at[k], rrecv.at[k], rs_sem.at[k], rr_sem.at[k], tok=dest(k)))

    groups = lh // GROUP
    last = groups - 1
    for g in range(groups):
        arrive(g)
        rows[g] = row_ids(g)
        cols[g] = jnp.broadcast_to(rows[g], (128, size)).T
        if g == last and sets == 1:
            break
        acc = one(g, 0)
        for b in range(1, g + 1):
            acc = acc + one(g, b)
        total[pl.ds(g * GROUP, GROUP)] = acc.reshape(GROUP, block, dom)
        for a in range(g):
            add(a, g)
    if sets > 1:
        for g in range(groups, n // GROUP):
            arrive(g)

        @pl.loop(groups, n // GROUP)
        def _(g):
            there = jnp.concatenate([srcs[g * GROUP + i] for i in range(GROUP)], axis=1)
            sb = pl.ds(g * GROUP, GROUP)
            for a in range(groups):
                sa = pl.ds(a * GROUP, GROUP)
                x = nt(part(recv[sa, 0]), part(recv[sb, 0])) * nt(part(recv[sa, 1]), part(recv[sb, 1]))
                col = jnp.broadcast_to(row_ids(a), (128, size)).T
                keep = jnp.concatenate([col] * (size // 128), axis=1) != there
                x = jnp.where(keep, x, 0.0).astype(BF16)
                y = jnp.dot(x, lall[sb].reshape(size, dom), preferred_element_type=F32)
                total[sa] += y.reshape(GROUP, block, dom)

    turn = sorted(range(groups), key=lambda a: (-(a.bit_length()), a))
    for i, a in enumerate(turn):
        if sets == 1:
            if a == last:
                acc = one(a, 0)
                for b in range(1, groups):
                    acc = acc + one(a, b)
                total[pl.ds(a * GROUP, GROUP)] = acc.reshape(GROUP, block, dom)
            else:
                add(a, last)
        swap(a)
        if i:
            owners(turn[i - 1])
    owners(turn[-1])
    acc = total[0, mine] + xrecv[0].astype(F32)
    for k in order[::-1]:
        back[k].wait_recv()
        acc = acc + rrecv[k].astype(F32)
    out[...] = acc * scale
    for copy in copies:
        copy.wait_send()


def on_device(acts, grads, losses, sources):
    block, lh, width = acts.shape
    dom = losses.shape[1]
    n = lax.axis_size("tok")
    layers = lh * lax.axis_size("lay")
    scale = 1.0 / math.sqrt(n * block * layers)
    half = block // 2
    dma = pltpu.SemaphoreType.DMA
    vmem = pl.BlockSpec(memory_space=pltpu.VMEM)
    pairs = n * block * block * lh
    return pl.pallas_call(
        functools.partial(kernel, n, lh, scale),
        out_shape=jax.ShapeDtypeStruct((half, dom), F32),
        in_specs=[pl.BlockSpec(memory_space=pl.ANY)] * 4,
        out_specs=vmem,
        scratch_shapes=[
            pltpu.VMEM((2, block, lh, width), BF16),
            pltpu.VMEM((2, block * lh, width), F32),
            pltpu.VMEM((lh, 2, block, width), BF16),
            pltpu.VMEM((n, 2, block, width), BF16),
            pltpu.VMEM((n, block, dom), BF16),
            pltpu.VMEM((n, 1, block), jnp.int32),
            pltpu.VMEM((lh, block, dom), F32),
            pltpu.VMEM((lh, half, dom), BF16),
            pltpu.VMEM((lh, half, dom), BF16),
            pltpu.VMEM((lh, half, dom), BF16),
            pltpu.VMEM((lh, half, dom), BF16),
            dma((n,)), dma((n,)), dma((n,)), dma((n,)), dma((n,)), dma((n,)), dma((n,)), dma((n,)), dma((n,)),
            dma((lh,)), dma((lh,)), dma((lh,)), dma((lh,)), dma((4,)),
        ],
        compiler_params=pltpu.CompilerParams(
            collective_id=0, has_side_effects=True, vmem_limit_bytes=56 * 1024 * 1024
        ),
        cost_estimate=pl.CostEstimate(
            flops=2 * pairs * (2 * width + dom), bytes_accessed=4 * block * lh * width, transcendentals=0
        ),
    )(acts, grads, losses, sources.reshape(1, block))


def solution(mesh):
    placed = (
        P(("grp", "tok"), "lay", None),
        P(("grp", "tok"), "lay", None),
        P(("grp", "tok"), None),
        P(("grp", "tok")),
    )
    return jax.shard_map(
        on_device,
        mesh=mesh,
        in_specs=placed,
        out_specs=P(("grp", "tok", "lay"), None),
        check_vma=False,
    )
```

```python
import functools
import math

import jax
import jax.numpy as jnp
from jax import lax
from jax.experimental import pallas as pl
from jax.experimental.pallas import tpu as pltpu
from jax.sharding import PartitionSpec as P

MESH = pl.DeviceIdType.MESH
F32 = jnp.float32
BF16 = jnp.bfloat16
GROUP = 2


def nt(a, b):
    return lax.dot_general(a, b, (((1,), (1,)), ((), ())), preferred_element_type=F32)


def kernel(
    n, lh, scale,
    acts, grads, losses, sources, out,
    fetched, stage, send, recv, lall, srcs, total, xsend, xrecv, rsend, rrecv,
    send_sem, recv_sem, ls_sem, lr_sem, lf_sem, lx_sem, ly_sem, ss_sem, sr_sem,
    xs_sem, xr_sem, rs_sem, rr_sem, in_sem,
):
    block = acts.shape[0]
    half = block // 2
    sets = n // lh
    me = lax.axis_index("tok")
    h = lax.axis_index("lay")
    q, j = me // lh, lax.rem(me, lh)

    def dest(k):
        return lax.rem(q + sets - k // lh, sets) * lh + jnp.bitwise_xor(j, k % lh)

    mine = pl.ds(pl.multiple_of(h * half, half), half)
    theirs = pl.ds(pl.multiple_of((1 - h) * half, half), half)
    peers = list(range(1, n))
    order = sorted(range(1, lh), key=lambda k: (-(k.bit_length()), k))
    send_order = [kq * lh + kj for kj in order for kq in range(sets)] + [kq * lh for kq in range(1, sets)]

    barrier = pltpu.get_barrier_semaphore()
    for k in peers:
        pl.semaphore_signal(barrier, inc=1, device_id={"tok": dest(k)}, device_id_type=MESH)
    pl.semaphore_signal(barrier, inc=1, device_id={"lay": 1 - h}, device_id_type=MESH)

    local = [
        pltpu.make_async_copy(src, dst, in_sem.at[i])
        for i, (src, dst) in enumerate(
            ((acts, fetched.at[0]), (grads, fetched.at[1]), (losses, lall.at[0]), (sources, srcs.at[0]))
        )
    ]
    for copy in local:
        copy.start()

    def cut(kj):
        layer = jnp.bitwise_xor(j, kj)
        for w in range(2):
            piece = stage[w, pl.ds(layer, block, stride=lh), :].astype(BF16)
            if kj == 0:
                recv[0, w] = piece
            if kj or sets > 1:
                send[kj, w] = piece

    ready = order[: lh // 2]
    for w in range(2):
        local[w].wait()
        stage[w] = fetched[w].astype(F32).reshape(block * lh, acts.shape[2])
    for kj in ready:
        cut(kj)
    for copy in local[2:]:
        copy.wait()
    pl.semaphore_wait(barrier, n)

    def remote(src, dst, s, r, **where):
        return pltpu.make_async_remote_copy(
            src_ref=src, dst_ref=dst, send_sem=s, recv_sem=r, device_id=where, device_id_type=MESH
        )

    copies = []

    def go(copy):
        copy.start()
        copies.append(copy)
        return copy

    first = {}
    for k in send_order:
        if k % 2 == 0:
            first[k] = go(remote(lall.at[0, mine], lall.at[k, mine], ls_sem.at[k], lr_sem.at[k], tok=dest(k)))
    first[1] = go(remote(lall.at[0, mine], lall.at[1, mine], ls_sem.at[1], lr_sem.at[1], tok=dest(1)))
    ids = {}
    for k in send_order:
        ids[k] = go(remote(srcs.at[0], srcs.at[k], ss_sem.at[k], sr_sem.at[k], tok=dest(k)))
    main = {}
    for kj in order + [0]:
        if kj not in ready:
            cut(kj)
        for kq in range(sets):
            k = kq * lh + kj
            if k:
                main[k] = go(remote(send.at[kj], recv.at[k], send_sem.at[k], recv_sem.at[k], tok=dest(k)))

    cross = {}
    for k in range(1, n):
        if k % 2 == 0:
            first[k].wait_recv()
            first[k + 1] = go(
                remote(lall.at[k, mine], lall.at[k + 1, mine], lf_sem.at[k + 1], lr_sem.at[k + 1], tok=dest(1))
            )
            cross[k] = go(remote(lall.at[k, mine], lall.at[k, mine], lx_sem.at[k], ly_sem.at[k], lay=1 - h))
    for k in range(1, n):
        if k % 2 == 1:
            first[k].wait_recv()
            cross[k] = go(remote(lall.at[k, mine], lall.at[k, mine], lx_sem.at[k], ly_sem.at[k], lay=1 - h))

    size = GROUP * block
    flat = (size, acts.shape[2])

    def part(ref_slice):
        return ref_slice.reshape(flat)

    def arrive(g):
        for k in range(g * GROUP, (g + 1) * GROUP):
            if k:
                main[k].wait_recv()
                ids[k].wait_recv()
                cross[k].wait_recv()

    def row_ids(g):
        return jnp.concatenate([srcs[g * GROUP + i] for i in range(GROUP)], axis=1)

    rows = {}
    cols = {}

    def one(a, b, both=False):
        sa, sb = pl.ds(a * GROUP, GROUP), pl.ds(b * GROUP, GROUP)
        x = nt(part(recv[sa, 0]), part(recv[sb, 0])) * nt(part(recv[sa, 1]), part(recv[sb, 1]))
        col = cols[a]
        reps = size // col.shape[1]
        keep = jnp.concatenate([col] * reps, axis=1) != rows[b]
        x = jnp.where(keep, x, 0.0).astype(BF16)
        y = jnp.dot(x, lall[sb].reshape(size, losses.shape[1]), preferred_element_type=F32)
        if not both:
            return y
        z = lax.dot_general(x, lall[sa].reshape(size, losses.shape[1]), (((0,), (0,)), ((), ())), preferred_element_type=F32)
        return y, z

    dom = losses.shape[1]

    def add(a, b):
        total[pl.ds(a * GROUP, GROUP)] += one(a, b).reshape(GROUP, block, dom)

    def full(g, after=None):
        acc = one(g, g)
        for a in sorted(range(g), key=lambda a: (-(a.bit_length()), a)):
            y, z = one(a, g, True)
            total[pl.ds(a * GROUP, GROUP)] += y.reshape(GROUP, block, dom)
            acc = acc + z
            if after and a == g - 1:
                after(a)
        total[pl.ds(g * GROUP, GROUP)] = acc.reshape(GROUP, block, dom)

    swaps = {}
    back = {}

    def swap(a):
        at = pl.ds(a * GROUP, GROUP)
        xsend[at] = total[at, theirs].astype(BF16)
        swaps[a] = go(remote(xsend.at[at], xrecv.at[at], xs_sem.at[a], xr_sem.at[a], lay=1 - h))

    def owners(a):
        swaps[a].wait_recv()
        for k in range(a * GROUP, (a + 1) * GROUP):
            if k:
                rsend[k] = (total[k, mine] + xrecv[k].astype(F32)).astype(BF16)
                back[k] = go(remote(rsend.at[k], rrecv.at[k], rs_sem.at[k], rr_sem.at[k], tok=dest(k)))

    groups = lh // GROUP
    last = groups - 1
    for g in range(groups):
        arrive(g)
        rows[g] = row_ids(g)
        cols[g] = jnp.broadcast_to(rows[g], (128, size)).T
        if g == last and sets == 1:
            break
        full(g)
    if sets > 1:
        for g in range(groups, n // GROUP):
            arrive(g)

        @pl.loop(groups, n // GROUP)
        def _(g):
            there = jnp.concatenate([srcs[g * GROUP + i] for i in range(GROUP)], axis=1)
            sb = pl.ds(g * GROUP, GROUP)
            for a in range(groups):
                sa = pl.ds(a * GROUP, GROUP)
                x = nt(part(recv[sa, 0]), part(recv[sb, 0])) * nt(part(recv[sa, 1]), part(recv[sb, 1]))
                col = jnp.broadcast_to(row_ids(a), (128, size)).T
                keep = jnp.concatenate([col] * (size // 128), axis=1) != there
                x = jnp.where(keep, x, 0.0).astype(BF16)
                y = jnp.dot(x, lall[sb].reshape(size, dom), preferred_element_type=F32)
                total[sa] += y.reshape(GROUP, block, dom)

    turn = sorted(range(groups), key=lambda a: (-(a.bit_length()), a))
    for i, a in enumerate(turn):
        if i == 0 and sets == 1:
            full(last, swap)
            for a in turn[1:]:
                swap(a)
        elif sets > 1:
            swap(a)
    for a in turn:
        owners(a)
    acc = total[0, mine] + xrecv[0].astype(F32)
    for k in order[::-1]:
        back[k].wait_recv()
        acc = acc + rrecv[k].astype(F32)
    out[...] = acc * scale
    for copy in copies:
        copy.wait_send()


def on_device(acts, grads, losses, sources):
    block, lh, width = acts.shape
    dom = losses.shape[1]
    n = lax.axis_size("tok")
    layers = lh * lax.axis_size("lay")
    scale = 1.0 / math.sqrt(n * block * layers)
    half = block // 2
    dma = pltpu.SemaphoreType.DMA
    vmem = pl.BlockSpec(memory_space=pltpu.VMEM)
    pairs = n * block * block * lh
    return pl.pallas_call(
        functools.partial(kernel, n, lh, scale),
        out_shape=jax.ShapeDtypeStruct((half, dom), F32),
        in_specs=[pl.BlockSpec(memory_space=pl.ANY)] * 4,
        out_specs=vmem,
        scratch_shapes=[
            pltpu.VMEM((2, block, lh, width), BF16),
            pltpu.VMEM((2, block * lh, width), F32),
            pltpu.VMEM((lh, 2, block, width), BF16),
            pltpu.VMEM((n, 2, block, width), BF16),
            pltpu.VMEM((n, block, dom), BF16),
            pltpu.VMEM((n, 1, block), jnp.int32),
            pltpu.VMEM((lh, block, dom), F32),
            pltpu.VMEM((lh, half, dom), BF16),
            pltpu.VMEM((lh, half, dom), BF16),
            pltpu.VMEM((lh, half, dom), BF16),
            pltpu.VMEM((lh, half, dom), BF16),
            dma((n,)), dma((n,)), dma((n,)), dma((n,)), dma((n,)), dma((n,)), dma((n,)), dma((n,)), dma((n,)),
            dma((lh,)), dma((lh,)), dma((lh,)), dma((lh,)), dma((4,)),
        ],
        compiler_params=pltpu.CompilerParams(
            collective_id=0, has_side_effects=True, vmem_limit_bytes=56 * 1024 * 1024
        ),
        cost_estimate=pl.CostEstimate(
            flops=2 * pairs * (2 * width + dom), bytes_accessed=4 * block * lh * width, transcendentals=0
        ),
    )(acts, grads, losses, sources.reshape(1, block))


def solution(mesh):
    placed = (
        P(("grp", "tok"), "lay", None),
        P(("grp", "tok"), "lay", None),
        P(("grp", "tok"), None),
        P(("grp", "tok")),
    )
    return jax.shard_map(
        on_device,
        mesh=mesh,
        in_specs=placed,
        out_specs=P(("grp", "tok", "lay"), None),
        check_vma=False,
    )
```
